32 devices in a mesh: occ: 8 (over z, y), virt: 4 (over x, core).
Axes of the slice: x: 2, y: 2, z: 4, core: 2. Of those that a mesh axis runs over, the one named last changes fastest.
Arguments:
- factors: bfloat16 [768, 98304], P('virt', 'occ'), may hold values from -1 to 1
- occ_energy: float32 [64], replicated, may hold values from -2 to -0.5
- virt_energy: float32 [768], replicated, may hold values from 0.2 to 3
- pair_table: int32 [16, 2], P('occ'), may hold values from 0 to 63, as said below
- pair_count: int32 [8], P('occ'), may hold values from 0 to 2, as said below
Outputs:
- gamma: float32 [768, 98304], P('virt', 'occ')
The draws below stay inside these ranges and needn't reach their ends.
Inputs may be any that keep to these rules, and one draw needn't show every extreme that they name: `pair_table`: each row holds two different orbitals. `pair_count`: the counts sum to exactly 8, and some host has exactly 2.
All inputs are finite; a program needn't handle non-finite values.
Results may differ from the reference program's by a relative error of at most 0.0029.
Values may be sent and summed in bfloat16 or wider, within the bound.
No kernel may reach another device: no remote copies, remote signals or barrier semaphores. Data moves between devices by JAX's collectives and lax.ppermute only.
A program may use at most 128 MiB of HBM per device.

```python
import jax
import jax.numpy as jnp
from jax import lax

O = 64
V = 768
NAUX = 1536
LOAD = 2
PAIRS = 8
N_OCC = 8


def draw_pair_table(key, part):
    key = jax.random.fold_in(key, 11)
    first_key, shift_key = jax.random.split(key)
    first = jax.random.randint(first_key, (N_OCC * LOAD,), 0, O)
    offset = jax.random.randint(shift_key, (N_OCC * LOAD,), 1, O)
    second = (first + offset) % O
    return jnp.stack([first, second], axis=1).astype(jnp.int32)


def draw_pair_count(key, part):
    key = jax.random.fold_in(key, 23)
    full_key, order_key = jax.random.split(key)
    busiest = jax.random.randint(full_key, (), 0, N_OCC)
    scores = jax.random.permutation(order_key, N_OCC * LOAD).astype(jnp.int32)
    slots = jnp.arange(N_OCC * LOAD, dtype=jnp.int32)
    owners = slots // LOAD
    scores = jnp.where(owners == busiest, slots % LOAD - LOAD, scores)
    ranking = jnp.argsort(jnp.argsort(scores, stable=True), stable=True)
    taken = (ranking < PAIRS).astype(jnp.int32)
    return jnp.sum(taken.reshape(N_OCC, LOAD), axis=1).astype(jnp.int32)


def steps_of(own_key, extent, cuts, smallest, top_value):
    factor_of, own = 1.0, jax.random.fold_in(own_key, 6)
    for dim, parts in cuts:
        heights = jnp.exp(jax.random.uniform(jax.random.fold_in(own, dim), (parts,), jnp.float32, smallest / len(cuts), top_value / len(cuts)))
        factor_of = factor_of * jnp.repeat(heights, extent[dim] // parts).reshape([-1 if axis == dim else 1 for axis in range(len(extent))])
    return factor_of


def normal_values(stream_key, extent, width, reach, cuts=(), kind=jnp.bfloat16):
    values = jax.random.normal(stream_key, extent, jnp.float32) * width
    if len(cuts) > 0:
        values = steps_of(stream_key, extent, cuts, -0.22, 0.18) * values
    return jnp.clip(values, min=-reach, max=reach).astype(kind)


def setup_inputs(seed: int = 0) -> dict:
    key_list = jax.random.split(jax.random.key(seed), 6)
    factors = normal_values(key_list[0], (V, NAUX * O), 0.16, 1.0, ((0, 4), (1, 8)))
    occ_energy = jnp.clip(jax.random.uniform(key_list[1], (O,), jnp.float32, -2.0, -0.5), -2.0, -0.5)
    virt_energy = jnp.clip(jax.random.uniform(key_list[2], (V,), jnp.float32, 0.2, 3.0), 0.2, 3.0)
    pair_table = draw_pair_table(jax.random.fold_in(key_list[5], 71), 0)
    pair_count = draw_pair_count(jax.random.fold_in(key_list[5], 71), 0)
    return dict(factors=factors, occ_energy=occ_energy, virt_energy=virt_energy, pair_table=pair_table, pair_count=pair_count)


def pair_terms(factors, occ_energy, virt_energy, first, second):
    left = lax.dynamic_index_in_dim(factors, first, 0, keepdims=False)
    right = lax.dynamic_index_in_dim(factors, second, 0, keepdims=False)
    couple = lax.dot_general(left, right, (((0,), (0,)), ((), ())), preferred_element_type=jnp.float32)
    energy_sum = jnp.take(occ_energy, first) + jnp.take(occ_energy, second)
    ampl = couple / (energy_sum - virt_energy[:, None] - virt_energy[None, :])
    mixed = (2.0 * ampl - ampl.T).astype(jnp.bfloat16)
    toward_first = lax.dot_general(right, mixed, (((1,), (1,)), ((), ())), preferred_element_type=jnp.float32)
    toward_second = jnp.dot(left, mixed, preferred_element_type=jnp.float32)
    return toward_first.astype(jnp.bfloat16), toward_second.astype(jnp.bfloat16)


def reference(factors, occ_energy, virt_energy, pair_table, pair_count):
    cube = factors.reshape(V, NAUX, O).transpose(2, 1, 0)
    entries = jnp.arange(N_OCC * LOAD, dtype=jnp.int32)
    active = (entries % LOAD) < jnp.repeat(pair_count, LOAD)
    ranking = jnp.cumsum(active.astype(jnp.int32)) - 1
    targets = jnp.arange(PAIRS, dtype=jnp.int32)
    select = (active[None, :] & (ranking[None, :] == targets[:, None])).astype(jnp.int32)
    chosen = jnp.sum(select[:, :, None] * pair_table[None, :, :], axis=1).astype(jnp.int32)

    def step(accumulated, row):
        first = row[0]
        second = row[1]
        toward_first, toward_second = pair_terms(cube, occ_energy, virt_energy, first, second)
        accumulated = accumulated.at[first].add(toward_first.astype(jnp.float32))
        accumulated = accumulated.at[second].add(toward_second.astype(jnp.float32))
        return accumulated, None

    start = jnp.zeros(cube.shape, jnp.float32)
    result, _ = lax.scan(step, start, chosen)
    return result.transpose(2, 1, 0).reshape(V, NAUX * O)
```

```python
import functools

import jax
import jax.numpy as jnp
from jax import lax
from jax.experimental import pallas as pl
from jax.experimental.pallas import tpu as pltpu
from jax.sharding import PartitionSpec as P

LANES = 128
STRIP = 16


def read_plan(tab_ref, me, hosts, per_host, first_ref, second_ref):
    for t in range(hosts):
        first_ref[t] = jnp.int32(-1)
        second_ref[t] = jnp.int32(-1)
    rank = jnp.int32(0)
    for h in range(hosts):
        slot = h ^ me
        count = tab_ref[slot, 2 * per_host]
        for r in range(per_host):
            live = (r < count) & (rank < hosts)

            @pl.when(live)
            def _(rank=rank, r=r, slot=slot):
                first_ref[rank] = tab_ref[slot, 2 * r]
                second_ref[rank] = tab_ref[slot, 2 * r + 1]

            rank = rank + live.astype(jnp.int32)


def pick_matrix(first_ref, second_ref, me, hosts, orbitals, sel_ref):
    width = STRIP * orbitals
    lane = lax.broadcasted_iota(jnp.int32, (STRIP, width), 1)
    row = lax.broadcasted_iota(jnp.int32, (STRIP, width), 0)
    here = lane - row * orbitals
    for s in range(hosts):
        for which, ref in enumerate((first_ref, second_ref)):
            orbital = ref[me ^ s]
            hit = (here == orbital) & (orbital >= 0)
            base = (which * hosts + s) * STRIP
            sel_ref[base:base + STRIP, :] = jnp.where(hit, 1.0, 0.0).astype(jnp.bfloat16)


def select_kernel(hosts, per_host, orbitals, strips, tab_ref, me_ref, x_ref, *rest):
    outs, (sel_ref, first_ref, second_ref) = rest[:hosts], rest[hosts:]
    me = me_ref[0]

    @pl.when(pl.program_id(0) == 0)
    def _():
        read_plan(tab_ref, me, hosts, per_host, first_ref, second_ref)
        pick_matrix(first_ref, second_ref, me, hosts, orbitals, sel_ref)

    width = STRIP * orbitals
    slab = x_ref.shape[0]
    for k in range(strips):
        picked = lax.dot_general(
            sel_ref[...], x_ref[:, k * width:(k + 1) * width], (((1,), (1,)), ((), ())),
            preferred_element_type=jnp.float32,
        ).astype(jnp.bfloat16)
        for s in range(hosts):
            left = picked[s * STRIP:(s + 1) * STRIP]
            right = picked[(hosts + s) * STRIP:(hosts + s + 1) * STRIP]
            outs[s][k * STRIP:(k + 1) * STRIP, :] = jnp.concatenate([left, right], axis=1)


def scatter_kernel(hosts, per_host, orbitals, strips, tab_ref, me_ref, *rest):
    ins, (out_ref, sel_ref, first_ref, second_ref) = rest[:hosts], rest[hosts:]
    me = me_ref[0]

    @pl.when(pl.program_id(0) == 0)
    def _():
        read_plan(tab_ref, me, hosts, per_host, first_ref, second_ref)
        pick_matrix(first_ref, second_ref, me, hosts, orbitals, sel_ref)

    width = STRIP * orbitals
    slab = out_ref.shape[0]
    for k in range(strips):
        rows = [ins[s][k * STRIP:(k + 1) * STRIP, :] for s in range(hosts)]
        stacked = jnp.concatenate([r[:, :slab] for r in rows] + [r[:, slab:] for r in rows], axis=0)
        out_ref[:, k * width:(k + 1) * width] = lax.dot_general(
            stacked, sel_ref[...], (((0,), (0,)), ((), ())), preferred_element_type=jnp.float32
        )


def pair_kernel(hosts, per_host, groups, step, tab_ref, me_ref, occ_ref, col_ref, row_ref, *rest):
    parts = rest[:groups]
    outs = rest[groups:groups + hosts]
    lall, rall, first_ref, second_ref = rest[groups + hosts:]
    me = me_ref[0]
    read_plan(tab_ref, me, hosts, per_host, first_ref, second_ref)
    i, j = first_ref[me], second_ref[me]
    live = jnp.where(i >= 0, 1.0, 0.0)
    energy = occ_ref[jnp.maximum(i, 0)] + occ_ref[jnp.maximum(j, 0)]
    slab = col_ref.shape[0]
    total, _ = lall.shape
    full = groups * slab

    def gather(c, carry):
        rows = pl.ds(pl.multiple_of(c * step, step), step)
        blocks = [parts[g][rows, :] for g in range(groups)]
        lall[rows, :] = jnp.concatenate([b[:, :slab] for b in blocks], axis=1)
        rall[rows, :] = jnp.concatenate([b[:, slab:] for b in blocks], axis=1)
        return carry

    lax.fori_loop(0, total // step, gather, 0)

    def couple(c, carry):
        one, two = carry
        rows = pl.ds(pl.multiple_of(c * step, step), step)
        dims = (((0,), (0,)), ((), ()))
        one = one + lax.dot_general(lall[rows, :slab], rall[rows, :], dims, preferred_element_type=jnp.float32)
        two = two + lax.dot_general(rall[rows, :slab], lall[rows, :], dims, preferred_element_type=jnp.float32)
        return one, two

    zero = jnp.zeros((slab, full), jnp.float32)
    one, two = lax.fori_loop(0, total // step, couple, (zero, zero))
    den = energy - col_ref[...] - row_ref[...]
    mixed_rows = (((2.0 * one - two) / den) * live).astype(jnp.bfloat16)
    mixed_cols = (((2.0 * two - one) / den) * live).astype(jnp.bfloat16)
    aux = total // hosts
    dims = (((1,), (1,)), ((), ()))
    for s in range(hosts):
        rows = slice(s * aux, (s + 1) * aux)
        toward_first = lax.dot_general(rall[rows, :], mixed_rows, dims, preferred_element_type=jnp.float32)
        toward_second = lax.dot_general(lall[rows, :], mixed_cols, dims, preferred_element_type=jnp.float32)
        outs[s][...] = jnp.concatenate(
            [toward_first.astype(jnp.bfloat16), toward_second.astype(jnp.bfloat16)], axis=1
        )


def fast_body(hosts, columns, factors, occ_energy, virt_energy, pair_table, pair_count):
    slab, local = factors.shape
    orbitals = occ_energy.shape[0]
    aux = local // orbitals
    per_host = pair_table.shape[0]
    me = lax.axis_index("occ").astype(jnp.int32)
    column = lax.axis_index("virt").astype(jnp.int32)
    vmem, smem = pltpu.VMEM, pltpu.SMEM

    table = jnp.concatenate([pair_table.reshape(1, -1), pair_count.reshape(1, 1)], axis=1)
    shift = 1
    while shift < hosts:
        other = lax.ppermute(table, "occ", [(d, d ^ shift) for d in range(hosts)])
        table = jnp.concatenate([table, other], axis=0)
        shift *= 2
    here = me.reshape(1)

    strips = 2 if aux % (2 * STRIP) == 0 else 1
    block = strips * STRIP
    width = block * orbitals
    steps = aux // block
    plan_scratch = [pltpu.SMEM((hosts,), jnp.int32), pltpu.SMEM((hosts,), jnp.int32)]
    sel_scratch = pltpu.VMEM((2 * hosts * STRIP, STRIP * orbitals), jnp.bfloat16)
    in_smem = pl.BlockSpec(memory_space=smem)
    in_vmem = pl.BlockSpec(memory_space=vmem)

    sent = pl.pallas_call(
        functools.partial(select_kernel, hosts, per_host, orbitals, strips),
        grid=(steps,),
        out_shape=[jax.ShapeDtypeStruct((aux, 2 * slab), jnp.bfloat16)] * hosts,
        in_specs=[in_smem, in_smem, pl.BlockSpec((slab, width), lambda g: (0, g))],
        out_specs=[pl.BlockSpec((block, 2 * slab), lambda g: (g, 0))] * hosts,
        scratch_shapes=[sel_scratch] + plan_scratch,
        name="select",
    )(table, here, factors)

    def exchange(pieces):
        got = {0: pieces[0]}
        for s in sorted(range(1, hosts), reverse=True):
            got[s] = lax.ppermute(pieces[s], "occ", [(d, d ^ s) for d in range(hosts)])
        return [got[s] for s in range(hosts)]

    arrived = exchange(sent)
    mine = jnp.concatenate(arrived, axis=0)
    parts = [mine]
    shift = columns // 2
    order = [0]
    while shift >= 1:
        parts = parts + [lax.ppermute(p, "virt", [(d, d ^ shift) for d in range(columns)]) for p in parts]
        order = order + [o ^ shift for o in order]
        shift //= 2
    energies = virt_energy.reshape(columns, slab)
    row = jnp.concatenate(
        [lax.dynamic_slice_in_dim(energies, column ^ o, 1, 0) for o in order], axis=1
    )
    col = lax.dynamic_slice_in_dim(energies, column, 1, 0).reshape(slab, 1)

    total = aux * hosts
    step = next(c for c in (256, 128, 64, 32, 16) if total % c == 0)
    toward = pl.pallas_call(
        functools.partial(pair_kernel, hosts, per_host, columns, step),
        out_shape=[jax.ShapeDtypeStruct((aux, 2 * slab), jnp.bfloat16)] * hosts,
        in_specs=[in_smem, in_smem, in_smem, in_vmem, in_vmem] + [in_vmem] * columns,
        out_specs=[in_vmem] * hosts,
        scratch_shapes=[pltpu.VMEM((total, columns * slab), jnp.bfloat16)] * 2 + plan_scratch,
        name="pairs",
    )(table, here, occ_energy, col, row, *parts)

    returned = exchange(toward)
    return pl.pallas_call(
        functools.partial(scatter_kernel, hosts, per_host, orbitals, strips),
        grid=(steps,),
        out_shape=jax.ShapeDtypeStruct((slab, local), jnp.float32),
        in_specs=[in_smem, in_smem] + [pl.BlockSpec((block, 2 * slab), lambda g: (g, 0))] * hosts,
        out_specs=pl.BlockSpec((slab, width), lambda g: (0, g)),
        scratch_shapes=[sel_scratch] + plan_scratch,
        name="scatter",
    )(table, here, *returned)


def plain_body(hosts, columns, factors, occ_energy, virt_energy, pair_table, pair_count):
    per_host = pair_table.shape[0]
    tables = lax.all_gather(pair_table, "occ", axis=0, tiled=True)
    counts = lax.all_gather(pair_count, "occ", axis=0, tiled=True)
    entries = jnp.arange(hosts * per_host, dtype=jnp.int32)
    active = entries % per_host < jnp.repeat(counts, per_host)
    slot_count = -(-(per_host * hosts // 2) // hosts)
    ranking = jnp.cumsum(active.astype(jnp.int32)) - 1
    targets = jnp.arange(hosts * slot_count, dtype=jnp.int32)
    select = (active[None, :] & (ranking[None, :] == targets[:, None])).astype(jnp.int32)
    plan = jnp.sum(select[:, :, None] * tables[None, :, :], axis=1).reshape(hosts, slot_count, 2)
    enabled = jnp.max(select, axis=1).reshape(hosts, slot_count)
    column = lax.axis_index("virt")
    myself = lax.axis_index("occ")
    orbitals = occ_energy.shape[0]
    slab = factors.shape[0]
    aux = factors.shape[1] // orbitals
    own = lax.dynamic_slice_in_dim(virt_energy, column * slab, slab)
    cube = factors.reshape(slab, aux, orbitals)
    gamma = jnp.zeros((slab, aux, orbitals), jnp.float32)
    for position in range(slot_count):
        wanted = plan[:, position].T.reshape(-1)
        onehot = (wanted[:, None] == jnp.arange(orbitals, dtype=jnp.int32)[None, :]).astype(jnp.bfloat16)
        picked = lax.dot_general(
            cube, onehot, (((2,), (1,)), ((), ())), preferred_element_type=jnp.float32
        ).astype(jnp.bfloat16)
        outgoing = picked.reshape(slab, aux, 2, hosts)
        both = lax.all_to_all(outgoing, "occ", split_axis=3, concat_axis=1, tiled=True)
        both = lax.all_gather(both, "virt", axis=0, tiled=True)
        left, right = both[:, :, 0, 0], both[:, :, 1, 0]
        mine = lax.dynamic_index_in_dim(plan[:, position], myself, 0, keepdims=False)
        live = lax.dynamic_index_in_dim(enabled[:, position], myself, 0, keepdims=False).astype(jnp.float32)
        left_slab = lax.dynamic_slice_in_dim(left, column * slab, slab, 0)
        right_slab = lax.dynamic_slice_in_dim(right, column * slab, slab, 0)
        dims = (((1,), (1,)), ((), ()))
        rows = lax.dot_general(left_slab, right, dims, preferred_element_type=jnp.float32)
        cols = lax.dot_general(right_slab, left, dims, preferred_element_type=jnp.float32)
        energy = jnp.take(occ_energy, mine[0]) + jnp.take(occ_energy, mine[1])
        den = energy - own[:, None] - virt_energy[None, :]
        mixed_rows = ((2.0 * rows - cols) / den * live).astype(jnp.bfloat16)
        mixed_cols = ((2.0 * cols - rows) / den * live).astype(jnp.bfloat16)
        toward_first = jnp.dot(mixed_rows, right, preferred_element_type=jnp.float32)
        toward_second = jnp.dot(mixed_cols, left, preferred_element_type=jnp.float32)
        packed = jnp.stack([toward_first.astype(jnp.bfloat16), toward_second.astype(jnp.bfloat16)], axis=2)
        packed = packed.reshape(slab, hosts, aux, 2, 1)
        back = lax.all_to_all(packed, "occ", split_axis=1, concat_axis=4, tiled=True)
        gamma = gamma + lax.dot_general(
            back.reshape(slab, aux, 2 * hosts), onehot, (((2,), (0,)), ((), ())), preferred_element_type=jnp.float32
        )
    return gamma.reshape(factors.shape)


def solution(mesh):
    hosts, columns = mesh.shape["occ"], mesh.shape["virt"]

    def body(factors, occ_energy, virt_energy, pair_table, pair_count):
        slab, local = factors.shape
        orbitals = occ_energy.shape[0]
        fits = (
            hosts <= 8
            and hosts & (hosts - 1) == 0
            and columns & (columns - 1) == 0
            and pair_table.shape[0] == 2
            and (local // orbitals) % STRIP == 0
            and (STRIP * orbitals) % LANES == 0
            and (2 * slab) % LANES == 0
        )
        run = fast_body if fits else plain_body
        return run(hosts, columns, factors, occ_energy, virt_energy, pair_table, pair_count)

    in_specs = (P("virt", "occ"), P(), P(), P("occ", None), P("occ"))
    return jax.shard_map(body, mesh=mesh, in_specs=in_specs, out_specs=P("virt", "occ"), check_vma=False)
```

```python
import functools

import jax
import jax.numpy as jnp
from jax import lax
from jax.experimental import pallas as pl
from jax.experimental.pallas import tpu as pltpu
from jax.sharding import PartitionSpec as P

LANES = 128
STRIP = 16
SELECT_BYTES = 24 * 1024 * 1024


def read_plan(tab_refs, me, hosts, per_host, first_ref, second_ref):
    tab_ref = tab_refs
    for t in range(hosts):
        first_ref[t] = jnp.int32(-1)
        second_ref[t] = jnp.int32(-1)
    rank = jnp.int32(0)
    for h in range(hosts):
        slot = h ^ me
        count = tab_ref[slot, 2 * per_host]
        for r in range(per_host):
            live = (r < count) & (rank < hosts)

            @pl.when(live)
            def _(rank=rank, r=r, slot=slot):
                first_ref[rank] = tab_ref[slot, 2 * r]
                second_ref[rank] = tab_ref[slot, 2 * r + 1]

            rank = rank + live.astype(jnp.int32)


def pick_matrix(first_ref, second_ref, me, hosts, orbitals, strip, sel_ref):
    width = strip * orbitals
    lane = lax.broadcasted_iota(jnp.int32, (strip, width), 1)
    row = lax.broadcasted_iota(jnp.int32, (strip, width), 0)
    here = lane - row * orbitals
    for s in range(hosts):
        for which, ref in enumerate((first_ref, second_ref)):
            orbital = ref[me ^ s]
            hit = (here == orbital) & (orbital >= 0)
            base = (which * hosts + s) * strip
            sel_ref[base:base + strip, :] = jnp.where(hit, 1.0, 0.0).astype(jnp.bfloat16)


def select_kernel(hosts, per_host, orbitals, tab_ref, ids_ref, x_ref, *rest):
    outs, (sel_ref, first_ref, second_ref) = rest[:hosts], rest[hosts:]
    me = ids_ref[0]
    read_plan(tab_ref, me, hosts, per_host, first_ref, second_ref)
    half = STRIP // 2
    pick_matrix(first_ref, second_ref, me, hosts, orbitals, half, sel_ref)
    width = half * orbitals
    aux = x_ref.shape[1] // orbitals
    for k in range(aux // STRIP):
        two = [
            lax.dot_general(
                sel_ref[...], x_ref[:, (2 * k + u) * width:(2 * k + u + 1) * width], (((1,), (1,)), ((), ())),
                preferred_element_type=jnp.float32,
            )
            for u in range(2)
        ]
        for s in range(hosts):
            left = jnp.concatenate([t[s * half:(s + 1) * half] for t in two], axis=0)
            right = jnp.concatenate([t[(hosts + s) * half:(hosts + s + 1) * half] for t in two], axis=0)
            outs[s][k * STRIP:(k + 1) * STRIP, :] = jnp.concatenate(
                [left.astype(jnp.bfloat16), right.astype(jnp.bfloat16)], axis=1
            )


def scatter_kernel(hosts, per_host, orbitals, strips, tab_ref, ids_ref, *rest):
    ins, (out_ref, sel_ref, first_ref, second_ref) = rest[:hosts], rest[hosts:]
    me = ids_ref[0]

    @pl.when(pl.program_id(0) == 0)
    def _():
        read_plan(tab_ref, me, hosts, per_host, first_ref, second_ref)
        pick_matrix(first_ref, second_ref, me, hosts, orbitals, STRIP, sel_ref)

    width = STRIP * orbitals
    slab = out_ref.shape[0]
    for k in range(strips):
        rows = [ins[s][k * STRIP:(k + 1) * STRIP, :] for s in range(hosts)]
        stacked = jnp.concatenate([r[:, :slab] for r in rows] + [r[:, slab:] for r in rows], axis=0)
        out_ref[:, k * width:(k + 1) * width] = lax.dot_general(
            stacked, sel_ref[...], (((0,), (0,)), ((), ())), preferred_element_type=jnp.float32
        )


def side_by_side(parts, rows, slab):
    blocks = [p[rows, :] for p in parts]
    return (
        jnp.concatenate([b[:, :slab] for b in blocks], axis=1),
        jnp.concatenate([b[:, slab:] for b in blocks], axis=1),
    )


def couple_chunks(parts, slab, step, one_ref, two_ref, lall=None, rall=None):
    dims = (((0,), (0,)), ((), ()))
    for c in range(parts[0].shape[0] // step):
        rows = slice(c * step, (c + 1) * step)
        left, right = side_by_side(parts, rows, slab)
        if lall is not None:
            lall[rows, :] = left
            rall[rows, :] = right
        one_ref[...] += lax.dot_general(left[:, :slab], right, dims, preferred_element_type=jnp.float32)
        two_ref[...] += lax.dot_general(right[:, :slab], left, dims, preferred_element_type=jnp.float32)


def toward_chunks(lefts, rights, mixed_rows, mixed_cols, out):
    dims = (((1,), (1,)), ((), ()))
    first = lax.dot_general(rights, mixed_rows, dims, preferred_element_type=jnp.float32)
    second = lax.dot_general(lefts, mixed_cols, dims, preferred_element_type=jnp.float32)
    out[...] = jnp.concatenate([first.astype(jnp.bfloat16), second.astype(jnp.bfloat16)], axis=1)


def near_kernel(groups, slab, step, *rest):
    parts, (one_ref, two_ref) = rest[:groups], rest[groups:]
    one_ref[...] = jnp.zeros_like(one_ref)
    two_ref[...] = jnp.zeros_like(two_ref)
    couple_chunks(parts, slab, step, one_ref, two_ref)


def far_kernel(hosts, per_host, order, slab, aux, step, tab_ref, ids_ref, occ_ref, virt_ref, one_in, two_in, *rest):
    groups = len(order)
    count = rest[0].shape[0] // aux
    parts, rest = rest[:groups], rest[groups:]
    outs, rest = rest[:count], rest[count:]
    rows_ref, cols_ref, one_ref, two_ref, lall, rall, first_ref, second_ref = rest
    me, column = ids_ref[0], ids_ref[1]
    read_plan(tab_ref, me, hosts, per_host, first_ref, second_ref)
    i, j = first_ref[me], second_ref[me]
    live = jnp.where(i >= 0, 1.0, 0.0)
    energy = occ_ref[jnp.maximum(i, 0)] + occ_ref[jnp.maximum(j, 0)]
    one_ref[...] = one_in[...]
    two_ref[...] = two_in[...]
    couple_chunks(parts, slab, step, one_ref, two_ref, lall, rall)
    bands = [virt_ref[:, g * slab:(g + 1) * slab] for g in range(groups)]

    def band(at):
        chosen = bands[0]
        for g in range(1, groups):
            chosen = jnp.where(at == g, bands[g], chosen)
        return chosen

    row = jnp.concatenate([band(column ^ o) for o in order], axis=1)
    col = jnp.transpose(jnp.broadcast_to(band(column), (LANES, slab)))[:, :1]
    den = energy - col - row
    one, two = one_ref[...], two_ref[...]
    rows_ref[...] = (((2.0 * one - two) / den) * live).astype(jnp.bfloat16)
    cols_ref[...] = (((2.0 * two - one) / den) * live).astype(jnp.bfloat16)
    for s in range(count):
        span = slice(s * aux, (s + 1) * aux)
        toward_chunks(lall[span, :], rall[span, :], rows_ref[...], cols_ref[...], outs[s])


def rest_kernel(groups, slab, aux, rows_ref, cols_ref, *rest):
    parts, outs = rest[:groups], rest[groups:]
    for s, out in enumerate(outs):
        left, right = side_by_side(parts, slice(s * aux, (s + 1) * aux), slab)
        toward_chunks(left, right, rows_ref[...], cols_ref[...], out)


def fast_body(hosts, columns, factors, occ_energy, virt_energy, pair_table, pair_count):
    slab, local = factors.shape
    orbitals = occ_energy.shape[0]
    aux = local // orbitals
    per_host = pair_table.shape[0]
    me = lax.axis_index("occ").astype(jnp.int32)
    column = lax.axis_index("virt").astype(jnp.int32)

    table = jnp.concatenate([pair_table.reshape(1, -1), pair_count.reshape(1, 1)], axis=1)
    shift = 1
    while shift < hosts:
        other = lax.ppermute(table, "occ", [(d, d ^ shift) for d in range(hosts)])
        table = jnp.concatenate([table, other], axis=0)
        shift *= 2
    ids = jnp.stack([me, column])

    plan_scratch = [pltpu.SMEM((hosts,), jnp.int32), pltpu.SMEM((hosts,), jnp.int32)]
    in_smem = pl.BlockSpec(memory_space=pltpu.SMEM)
    in_vmem = pl.BlockSpec(memory_space=pltpu.VMEM)
    piece = jax.ShapeDtypeStruct((aux, 2 * slab), jnp.bfloat16)
    bf16, f32 = jnp.bfloat16, jnp.float32
    full = columns * slab

    sent = pl.pallas_call(
        functools.partial(select_kernel, hosts, per_host, orbitals),
        out_shape=[piece] * hosts,
        in_specs=[in_smem, in_smem, in_vmem],
        out_specs=[in_vmem] * hosts,
        scratch_shapes=[pltpu.VMEM((hosts * STRIP, STRIP // 2 * orbitals), bf16)] + plan_scratch,
        compiler_params=pltpu.CompilerParams(vmem_limit_bytes=SELECT_BYTES),
        name="select",
    )(table, ids, factors)

    def over_occ(x, s):
        return lax.ppermute(x, "occ", [(d, d ^ s) for d in range(hosts)])

    def over_virt(x, s):
        return lax.ppermute(x, "virt", [(d, d ^ s) for d in range(columns)])

    def spread(x):
        parts, order = [x], [0]
        shift = columns // 2
        while shift >= 1:
            parts = parts + [over_virt(p, shift) for p in parts]
            order = order + [o ^ shift for o in order]
            shift //= 2
        return parts, order

    cut = hosts // 2
    got = {0: sent[0]}
    for s in reversed(range(1, hosts)):
        got[s] = over_occ(sent[s], s)
    near, order = spread(jnp.concatenate([got[s] for s in range(cut)], axis=0))
    far, _ = spread(jnp.concatenate([got[s] for s in range(cut, hosts)], axis=0))

    span = cut * aux
    step = next(c for c in (256, 128, 64, 32, 16) if span % c == 0)
    square = jax.ShapeDtypeStruct((slab, full), f32)
    flops = 4 * slab * full * span
    one, two = pl.pallas_call(
        functools.partial(near_kernel, columns, slab, step),
        out_shape=[square] * 2,
        in_specs=[in_vmem] * columns,
        out_specs=[in_vmem] * 2,
        cost_estimate=pl.CostEstimate(flops=flops, bytes_accessed=columns * span * slab * 4, transcendentals=0),
        name="near",
    )(*near)
    mixed = jax.ShapeDtypeStruct((slab, full), bf16)
    *late, mixed_rows, mixed_cols = pl.pallas_call(
        functools.partial(far_kernel, hosts, per_host, tuple(order), slab, aux, step),
        out_shape=[piece] * (hosts - cut) + [mixed] * 2,
        in_specs=[in_smem] * 3 + [in_vmem] * (3 + columns),
        out_specs=[in_vmem] * (hosts - cut + 2),
        scratch_shapes=[pltpu.VMEM((slab, full), f32)] * 2
        + [pltpu.VMEM((span, full), bf16)] * 2
        + plan_scratch,
        name="far",
    )(table, ids, occ_energy, virt_energy.reshape(1, full), one, two, *far)
    early = pl.pallas_call(
        functools.partial(rest_kernel, columns, slab, aux),
        out_shape=[piece] * cut,
        in_specs=[in_vmem] * (2 + columns),
        out_specs=[in_vmem] * cut,
        cost_estimate=pl.CostEstimate(flops=flops, bytes_accessed=columns * span * slab * 4, transcendentals=0),
        name="rest",
    )(mixed_rows, mixed_cols, *near)

    home = {}
    for s in reversed(range(cut, hosts)):
        home[s] = over_occ(late[s - cut], s)
    for s in reversed(range(1, cut)):
        home[s] = over_occ(early[s], s)
    home[0] = early[0]

    strips = next(c for c in (4, 3, 2, 1) if aux % (c * STRIP) == 0)
    block = strips * STRIP
    return pl.pallas_call(
        functools.partial(scatter_kernel, hosts, per_host, orbitals, strips),
        grid=(aux // block,),
        out_shape=jax.ShapeDtypeStruct((slab, local), f32),
        in_specs=[in_smem, in_smem] + [pl.BlockSpec((block, 2 * slab), lambda g: (g, 0))] * hosts,
        out_specs=pl.BlockSpec((slab, block * orbitals), lambda g: (0, g)),
        scratch_shapes=[pltpu.VMEM((2 * hosts * STRIP, STRIP * orbitals), bf16)] + plan_scratch,
        name="scatter",
    )(table, ids, *[home[s] for s in range(hosts)])


def plain_body(hosts, columns, factors, occ_energy, virt_energy, pair_table, pair_count):
    per_host = pair_table.shape[0]
    tables = lax.all_gather(pair_table, "occ", axis=0, tiled=True)
    counts = lax.all_gather(pair_count, "occ", axis=0, tiled=True)
    entries = jnp.arange(hosts * per_host, dtype=jnp.int32)
    active = entries % per_host < jnp.repeat(counts, per_host)
    slot_count = -(-(per_host * hosts // 2) // hosts)
    ranking = jnp.cumsum(active.astype(jnp.int32)) - 1
    targets = jnp.arange(hosts * slot_count, dtype=jnp.int32)
    select = (active[None, :] & (ranking[None, :] == targets[:, None])).astype(jnp.int32)
    plan = jnp.sum(select[:, :, None] * tables[None, :, :], axis=1).reshape(hosts, slot_count, 2)
    enabled = jnp.max(select, axis=1).reshape(hosts, slot_count)
    column = lax.axis_index("virt")
    myself = lax.axis_index("occ")
    orbitals = occ_energy.shape[0]
    slab = factors.shape[0]
    aux = factors.shape[1] // orbitals
    own = lax.dynamic_slice_in_dim(virt_energy, column * slab, slab)
    cube = factors.reshape(slab, aux, orbitals)
    gamma = jnp.zeros((slab, aux, orbitals), jnp.float32)
    for position in range(slot_count):
        wanted = plan[:, position].T.reshape(-1)
        onehot = (wanted[:, None] == jnp.arange(orbitals, dtype=jnp.int32)[None, :]).astype(jnp.bfloat16)
        picked = lax.dot_general(
            cube, onehot, (((2,), (1,)), ((), ())), preferred_element_type=jnp.float32
        ).astype(jnp.bfloat16)
        outgoing = picked.reshape(slab, aux, 2, hosts)
        both = lax.all_to_all(outgoing, "occ", split_axis=3, concat_axis=1, tiled=True)
        both = lax.all_gather(both, "virt", axis=0, tiled=True)
        left, right = both[:, :, 0, 0], both[:, :, 1, 0]
        mine = lax.dynamic_index_in_dim(plan[:, position], myself, 0, keepdims=False)
        live = lax.dynamic_index_in_dim(enabled[:, position], myself, 0, keepdims=False).astype(jnp.float32)
        left_slab = lax.dynamic_slice_in_dim(left, column * slab, slab, 0)
        right_slab = lax.dynamic_slice_in_dim(right, column * slab, slab, 0)
        dims = (((1,), (1,)), ((), ()))
        rows = lax.dot_general(left_slab, right, dims, preferred_element_type=jnp.float32)
        cols = lax.dot_general(right_slab, left, dims, preferred_element_type=jnp.float32)
        energy = jnp.take(occ_energy, mine[0]) + jnp.take(occ_energy, mine[1])
        den = energy - own[:, None] - virt_energy[None, :]
        mixed_rows = ((2.0 * rows - cols) / den * live).astype(jnp.bfloat16)
        mixed_cols = ((2.0 * cols - rows) / den * live).astype(jnp.bfloat16)
        toward_first = jnp.dot(mixed_rows, right, preferred_element_type=jnp.float32)
        toward_second = jnp.dot(mixed_cols, left, preferred_element_type=jnp.float32)
        packed = jnp.stack([toward_first.astype(jnp.bfloat16), toward_second.astype(jnp.bfloat16)], axis=2)
        packed = packed.reshape(slab, hosts, aux, 2, 1)
        back = lax.all_to_all(packed, "occ", split_axis=1, concat_axis=4, tiled=True)
        gamma = gamma + lax.dot_general(
            back.reshape(slab, aux, 2 * hosts), onehot, (((2,), (0,)), ((), ())), preferred_element_type=jnp.float32
        )
    return gamma.reshape(factors.shape)


def solution(mesh):
    hosts, columns = mesh.shape["occ"], mesh.shape["virt"]

    def body(factors, occ_energy, virt_energy, pair_table, pair_count):
        slab, local = factors.shape
        orbitals = occ_energy.shape[0]
        fits = (
            hosts <= 8
            and hosts & (hosts - 1) == 0
            and columns & (columns - 1) == 0
            and pair_table.shape[0] == 2
            and (local // orbitals) % STRIP == 0
            and (STRIP * orbitals) % LANES == 0
            and (2 * slab) % LANES == 0
        )
        run = fast_body if fits else plain_body
        return run(hosts, columns, factors, occ_energy, virt_energy, pair_table, pair_count)

    in_specs = (P("virt", "occ"), P(), P(), P("occ", None), P("occ"))
    return jax.shard_map(body, mesh=mesh, in_specs=in_specs, out_specs=P("virt", "occ"), check_vma=False)
```
